256 devices in a mesh: dp: 64 (over x, z, core), rep: 4 (over y).
Axes of the slice: x: 4, y: 4, z: 8, core: 2. Of those that a mesh axis runs over, the one named last changes fastest.
Arguments:
- frames_in: bfloat16 [4, 57344, 1536], P('rep', 'dp')
- lengths: int32 [4, 64, 4], P('rep', 'dp'), may hold values from 1 to 893, as said below
- norm_gain: float32 [1536], replicated, may hold values from 0.5 to 1.5
- norm_bias: float32 [1536], replicated, may hold values from -2 to 2
- w_in: bfloat16 [1536, 3072], P(('dp', 'rep')), may hold values from -0.15625 to 0.15625
- kernel: float32 [31, 1536], replicated, may hold values from -1 to 1
- batch_gain: float32 [1536], replicated, may hold values from 0.5 to 1.5
- batch_bias: float32 [1536], replicated, may hold values from -3 to 3
- w_out: bfloat16 [1536, 1536], P(('dp', 'rep')), may hold values from -0.15625 to 0.15625
Outputs:
- frames_out: bfloat16 [4, 57344, 1536], P('rep', 'dp')
The draws below stay inside these ranges and needn't reach their ends.
Inputs may be any that keep to these rules, and one draw needn't show every extreme that they name: `lengths`: for each rep index, the devices 2k and 2k + 1 of dp hold 1024 frames together, so each rep index holds 512 frames for each of its dp devices; a device holds at most 896 frames, and some device of every rep index holds exactly 896.
All inputs are finite; a program needn't handle non-finite values.
Results may differ from the reference program's by a relative error of at most 0.0038.
Values may be sent and summed in bfloat16 or wider, within the bound.
A program may use at most 128 MiB of HBM per device.

```python
import jax
import jax.numpy as jnp
from jax import lax

D = 1536
FR_DEV = 512
UPD = 4
KERNEL = 31
CAP = 896
N_DP = 64
N_REP = 4


def draw_frames_in(key, part):
    noise_key, pattern_key = jax.random.split(key, 2)
    holder = jnp.arange(N_DP * CAP, dtype=jnp.int32) // CAP
    ramp = 3.0 * holder.astype(jnp.float32) / (N_DP - 1)
    pattern = jax.random.normal(pattern_key, (D,), jnp.float32)
    noise = jax.random.normal(noise_key, (N_REP, N_DP * CAP, D), jnp.float32)
    values = noise + ramp[None, :, None] * pattern[None, None, :]
    return values.astype(jnp.bfloat16)


def draw_lengths(key, part):
    pair_count = N_DP // 2
    surplus = 3 * FR_DEV // 4
    shift_key, chosen_key, heavy_key, piece_key = jax.random.split(key, 4)
    shifts = jax.random.randint(shift_key, (N_REP, pair_count), 0, surplus + 1, jnp.int32)
    chosen = jax.random.randint(chosen_key, (N_REP, 1), 0, pair_count, jnp.int32)
    shifts = jnp.where(jnp.arange(pair_count, dtype=jnp.int32)[None, :] == chosen, surplus, shifts)
    heavy = jax.random.randint(heavy_key, (N_REP, pair_count), 0, 2, jnp.int32) * 2 - 1
    first_load = FR_DEV + heavy * shifts
    device_load = jnp.stack([first_load, 2 * FR_DEV - first_load], axis=2).reshape(N_REP, N_DP)
    lower = device_load // (2 * UPD)
    upper = device_load // UPD + 1
    pieces = jax.random.randint(piece_key, (N_REP, N_DP, UPD - 1), lower[:, :, None], upper[:, :, None], jnp.int32)
    full_device = (device_load == CAP)[:, :, None]
    pieces = jnp.where(full_device, jnp.ones_like(pieces), pieces)
    remainder = device_load - jnp.sum(pieces, axis=2)
    return jnp.concatenate([pieces, remainder[:, :, None]], axis=2).astype(jnp.int32)


def level_of(stream_key, dims, cuts, low, high):
    level = 1.0
    for dim, parts in cuts:
        heights = jax.random.uniform(jax.random.fold_in(jax.random.fold_in(stream_key, 6), dim), (parts,), jnp.float32, low / len(cuts), high / len(cuts))
        level = level * jnp.repeat(jnp.exp(heights), dims[dim] // parts).reshape((-1,) + (1,) * (len(dims) - 1 - dim))
    return level


def gaussian(own_key, dims, scale, limit, shards=(), kind=jnp.bfloat16):
    drawn = scale * jax.random.normal(own_key, dims, jnp.float32)
    if shards:
        drawn = drawn * level_of(own_key, dims, shards, -0.22, 0.18)
    return jnp.clip(drawn, -limit, limit).astype(kind)


def setup_inputs(seed: int = 0) -> dict:
    splits = jax.random.split(jax.random.key(seed), 10)
    return {
        "frames_in": draw_frames_in(jax.random.fold_in(splits[9], 71), 0),
        "lengths": draw_lengths(jax.random.fold_in(splits[9], 71), 0),
        "norm_gain": jnp.clip(1.0 + 0.1 * jax.random.normal(splits[2], (D,), jnp.float32), 0.5, 1.5),
        "norm_bias": gaussian(splits[3], (D,), 0.3, 2.0, (), jnp.float32),
        "w_in": gaussian(splits[4], (D, 2 * D), D ** -0.5, 0.15625, ((0, 256),)),
        "kernel": gaussian(splits[5], (KERNEL, D), KERNEL ** -0.5, 1.0, (), jnp.float32),
        "batch_gain": jnp.clip(1.0 + 0.1 * jax.random.normal(splits[6], (D,), jnp.float32), 0.5, 1.5),
        "batch_bias": gaussian(splits[7], (D,), 0.5, 3.0, (), jnp.float32),
        "w_out": gaussian(splits[8], (D, D), D ** -0.5, 0.15625, ((0, 256),)),
    }


EPSILON = 1e-05

def layer_norm(frames, norm_gain, norm_bias):
    values = frames.astype(jnp.float32)
    average = lax.optimization_barrier(jnp.mean(values, axis=-1, keepdims=True))
    centred = values - average
    spread = lax.optimization_barrier(jnp.mean(centred * centred, axis=-1, keepdims=True))
    return centred * lax.rsqrt(spread + EPSILON) * norm_gain + norm_bias

def depthwise(gated, labels, kernel):
    half_kernel = kernel.shape[0] // 2
    length_rows = gated.shape[0]
    padded = jnp.pad(gated.astype(jnp.float32), ((half_kernel, half_kernel), (0, 0)))
    padded_labels = jnp.pad(labels, (half_kernel, half_kernel), constant_values=-1)
    summed = jnp.zeros(gated.shape, jnp.float32)
    for offset in range(kernel.shape[0]):
        shared = padded_labels[offset:offset + length_rows] == labels
        contribution = jnp.where(shared[:, None], padded[offset:offset + length_rows], 0.0)
        summed = summed + contribution * kernel[offset]
    return summed

def pack_group(group_lengths):
    device_load = lax.optimization_barrier(jnp.sum(group_lengths, axis=1)).astype(jnp.int32)
    offsets = (jnp.cumsum(device_load) - device_load).astype(jnp.int32)
    packed = jnp.arange(N_DP * FR_DEV, dtype=jnp.int32)
    holder = lax.optimization_barrier(jnp.sum((packed[:, None] >= offsets[None, 1:]).astype(jnp.int32), axis=1)).astype(jnp.int32)
    within = (packed - offsets[holder]).astype(jnp.int32)
    source = (holder * CAP + within).astype(jnp.int32)
    boundary = jnp.cumsum(group_lengths, axis=1).astype(jnp.int32)
    utterance = holder * UPD + lax.optimization_barrier(jnp.sum((within[:, None] >= boundary[holder]).astype(jnp.int32), axis=1)).astype(jnp.int32)
    return (source, utterance.astype(jnp.int32))

def reference(frames_in, lengths, norm_gain, norm_bias, w_in, kernel, batch_gain, batch_bias, w_out):

    def first_pass(operands):
        block_frames, group_lengths = operands
        source, utterance = pack_group(group_lengths)
        packed = block_frames[source]
        normed = layer_norm(packed, norm_gain, norm_bias).astype(jnp.bfloat16)
        projected = jnp.dot(normed, w_in, preferred_element_type=jnp.float32)
        gated = (projected[:, :D] * jax.nn.sigmoid(projected[:, D:])).astype(jnp.bfloat16)
        return depthwise(gated, utterance, kernel)
    convolved = lax.map(first_pass, (frames_in, lengths))
    total_count = N_REP * N_DP * FR_DEV
    average = lax.optimization_barrier(jnp.sum(convolved, axis=(0, 1))) / total_count
    spread = lax.optimization_barrier(jnp.sum(jnp.square(convolved - average), axis=(0, 1))) / total_count

    def second_pass(operands):
        block_frames, group_lengths, group_conv = operands
        source, utterance = pack_group(group_lengths)
        scaled = (group_conv - average) * lax.rsqrt(spread + EPSILON) * batch_gain + batch_bias
        active = jax.nn.silu(scaled).astype(jnp.bfloat16)
        branch = jnp.dot(active, w_out, preferred_element_type=jnp.float32)
        mixed = (block_frames[source].astype(jnp.float32) + branch).astype(jnp.bfloat16)
        return jnp.zeros((N_DP * CAP, D), jnp.bfloat16).at[source].set(mixed)
    return lax.map(second_pass, (frames_in, lengths, convolved))
```

```python
import functools

import jax
import jax.numpy as jnp
import numpy as np
from jax import lax
from jax.experimental import pallas as pl
from jax.experimental.pallas import tpu as pltpu
from jax.sharding import PartitionSpec as P

EPSILON = 1e-05
MESH = pl.DeviceIdType.MESH
F32 = jnp.float32
BF16 = jnp.bfloat16

NX, NY, NZ, NC = 4, 4, 8, 2
D = 1536
HALF = D // 2
CAP = 896
PAIR = 1024
GAP = 15
ROWS = 1152
BLK = 128
NB = ROWS // BLK
WIN = 192
TAPS = 31
N_IN = 6
N_OUT = 3
NCH = N_IN + N_OUT
TOTAL = 512 * 256


def feature_order():
    order = np.zeros((384, 384), np.float32)
    for z in range(8):
        for c in range(2):
            for y in range(4):
                for i in range(6):
                    order[z * 48 + c * 24 + y * 6 + i, y * 96 + z * 12 + c * 6 + i] = 1.0
    return order


def compaction():
    pick = np.zeros((96, 128), np.float32)
    for k in range(16):
        for i in range(6):
            pick[k * 6 + i, k * 8 + i] = 1.0
    return pick


def kernel(
    lengths_ref, x_ref, gain_ref, bias_ref, w_in_ref, w_out_ref, taps_ref, bgain_ref, bbias_ref,
    order_ref, pick_ref,
    out_ref,
    slab, zin, weights, xs, normed_own, normed_mate, mask_own, mask_mate,
    proj, gated, conv, act, w_nat, st_own, st_a, st_b0, st_b, stats,
    z_send, z_recv, ring_send, r1_recv, r2_recv, n_send, n_recv, m_send, m_recv,
    c_send, c_recv, w_send, w_recv, sa_send, sa_recv, sb_send, sb_recv,
):
    dp = lax.axis_index("dp")
    y = lax.axis_index("rep")
    x = dp // 16
    z = lax.rem(dp // 2, 8)
    c = lax.rem(dp, 2)
    mate = (x * 16 + z * 2 + (1 - c), y)

    def device(xx, yy, zz, cc):
        return (lax.rem(xx + 4, 4) * 16 + lax.rem(zz + 8, 8) * 2 + cc, lax.rem(yy + 4, 4))

    def z_peer(k):
        me = z * 2 + c
        other = lax.rem(me + k, 16)
        return other // 2, lax.rem(other, 2)

    def xy_peer(k):
        me = x * 4 + y
        other = lax.rem(me + k, 16)
        return other // 4, lax.rem(other, 4)

    barrier = pltpu.get_barrier_semaphore()

    def greet(k, carry):
        zz, cc = z_peer(k)
        pl.semaphore_signal(barrier, 1, device_id=device(x, y, zz, cc), device_id_type=MESH)
        xx, yy = xy_peer(k)
        pl.semaphore_signal(barrier, 1, device_id=device(xx, yy, z, c), device_id_type=MESH)
        return carry

    lax.fori_loop(1, 16, greet, 0)

    slab[...] = jnp.zeros_like(slab)
    for h in range(2):
        for j in range(N_IN):
            lo = h * HALF + j * 128
            slab[h, j, 0:6, 0:128] = w_in_ref[:, lo : lo + 128]
            slab[h, j, 0:6, 128:256] = w_in_ref[:, D + lo : D + lo + 128]
        for j in range(N_OUT):
            lo = h * HALF + j * 256
            slab[h, N_IN + j, 0:6, :] = w_out_ref[:, lo : lo + 256]
    for j in range(NCH):
        zin[j, z * 2 + c] = slab[c, j]

    pl.semaphore_wait(barrier, 30)

    def z_start(j):
        def one(k, carry):
            zz, cc = z_peer(k)
            pltpu.make_async_remote_copy(
                src_ref=slab.at[cc, j], dst_ref=zin.at[j, z * 2 + c],
                send_sem=z_send, recv_sem=z_recv.at[j],
                device_id=device(x, y, zz, cc), device_id_type=MESH,
            ).start()
            return carry
        lax.fori_loop(1, 16, one, 0)

    def wait_for(ref, sem):
        pltpu.make_async_copy(ref, ref, sem).wait()

    def first_axis(j):
        f = lax.rem(c + j, 2)
        d = 1 - 2 * lax.rem(j // 2, 2)
        return f, d

    def along(f, step):
        return x + (1 - f) * step, y + f * step

    def ring1_copy(j, f, origin, to, slot):
        ox, oy = along(f, origin)
        tx, ty = along(f, to)
        ref = weights.at[j * 16 + lax.rem(ox + 4, 4) * 4 + lax.rem(oy + 4, 4)]
        pltpu.make_async_remote_copy(
            src_ref=ref, dst_ref=ref, send_sem=ring_send, recv_sem=r1_recv.at[j, slot],
            device_id=device(tx, ty, z, c), device_id_type=MESH,
        ).start()

    def ring2_copy(j, f, origin, to, slot):
        s = 1 - f
        ox, oy = along(s, origin)
        tx, ty = along(s, to)
        ox, oy = lax.rem(ox + 4, 4), lax.rem(oy + 4, 4)
        for k in range(4):
            ref = weights.at[j * 16 + jnp.where(f == 0, k * 4 + oy, ox * 4 + k)]
            pltpu.make_async_remote_copy(
                src_ref=ref, dst_ref=ref, send_sem=ring_send, recv_sem=r2_recv.at[j, slot],
                device_id=device(tx, ty, z, c), device_id_type=MESH,
            ).start()

    def e1(j):
        wait_for(zin.at[0, pl.ds(0, 15)], z_recv.at[j])
        rows = zin[j].reshape(128, 256)
        block = jnp.dot(pick_ref[...], rows, preferred_element_type=F32).astype(BF16)
        weights[j * 16 + x * 4 + y] = block
        f, _ = first_axis(j)
        ring1_copy(j, f, 0, 1, 0)
        ring1_copy(j, f, 0, -1, 1)

    def e2(j):
        f, d = first_axis(j)
        wait_for(weights.at[0], r1_recv.at[j, 0])
        wait_for(weights.at[0], r1_recv.at[j, 1])
        ring1_copy(j, f, -d, d, 2)

    def e3(j):
        f, _ = first_axis(j)
        wait_for(weights.at[0], r1_recv.at[j, 2])
        ring2_copy(j, f, 0, 1, 0)
        ring2_copy(j, f, 0, -1, 1)

    def e4(j):
        f, d = first_axis(j)
        wait_for(weights.at[pl.ds(0, 4)], r2_recv.at[j, 0])
        wait_for(weights.at[pl.ds(0, 4)], r2_recv.at[j, 1])
        ring2_copy(j, f, -d, d, 2)

    def e5(j):
        wait_for(weights.at[pl.ds(0, 4)], r2_recv.at[j, 2])

    n_own = lengths_ref[0] + lengths_ref[1] + lengths_ref[2] + lengths_ref[3]
    b0 = lengths_ref[0]
    b1 = b0 + lengths_ref[1]
    b2 = b1 + lengths_ref[2]
    base = c * (PAIR - n_own + 4 * GAP)

    def place(i):
        u = (i >= b0).astype(jnp.int32) + (i >= b1).astype(jnp.int32) + (i >= b2).astype(jnp.int32)
        return i + base + GAP * u

    def window(ref, w):
        return jnp.concatenate([ref[w + k] for k in range(WIN // 16)], axis=0)

    def layer_norm_block(qi):
        q = qi + c
        low = jnp.maximum(q * BLK - base - 3 * GAP, 0)
        w = jnp.minimum(lax.div(low, 16), (CAP - WIN) // 16)
        i = w * 16 + lax.broadcasted_iota(jnp.int32, (BLK, WIN), 1)
        r = q * BLK + lax.broadcasted_iota(jnp.int32, (BLK, WIN), 0)
        chosen = jnp.logical_and(place(i) == r, i < n_own).astype(F32)
        xs[...] = jnp.dot(chosen.astype(BF16), window(x_ref, w), preferred_element_type=F32)
        live = jnp.broadcast_to(jnp.sum(chosen, axis=1, keepdims=True), (BLK, 128))
        mask_own[q] = live

        def rows(g, carry):
            at = pl.ds(pl.multiple_of(g * 16, 16), 16)
            v = xs[at, :]
            average = jnp.sum(v, axis=1, keepdims=True) * (1.0 / D)
            centred = v - average
            spread = jnp.sum(centred * centred, axis=1, keepdims=True) * (1.0 / D)
            res = centred * lax.rsqrt(spread + EPSILON) * gain_ref[...] + bias_ref[...]
            m = mask_own[q, at, 0:1]
            normed_own[q, at, :] = jnp.where(m > 0.0, res, 0.0).astype(BF16)
            return carry

        lax.fori_loop(0, BLK // 16, rows, 0)
        for g in range(4):
            cols = slice(g * 384, (g + 1) * 384)
            normed_own[q, :, cols] = jnp.dot(
                normed_own[q, :, cols], order_ref[...], preferred_element_type=F32
            ).astype(BF16)
        pltpu.make_async_remote_copy(
            src_ref=normed_own.at[q], dst_ref=normed_mate.at[q], send_sem=n_send, recv_sem=n_recv,
            device_id=mate, device_id_type=MESH,
        ).start()

    def project(j):
        w = weights[pl.ds(j * 16, 16)].reshape(D, 256)

        def rows(b, carry):
            at = pl.ds(b * 3, 3)
            proj[...] = jnp.dot(
                normed_own[at].reshape(3 * BLK, D), w, preferred_element_type=F32
            )
            v = proj[:, 0:128]
            g = proj[:, 128:256]
            res = v * jax.nn.sigmoid(g)
            gated[pl.ds(pl.multiple_of(16 + b * 3 * BLK, 16), 3 * BLK), :] = res.astype(BF16).astype(F32)
            return carry

        lax.fori_loop(0, NB // 3, rows, 0)

    def convolve(j):
        cc = c * N_IN + j
        lanes = pl.ds(pl.multiple_of(cc * 128, 128), 128)
        taps = taps_ref[:, lanes]

        def rows(b, total):
            r0 = pl.multiple_of(b * BLK, BLK)
            v = gated[pl.ds(r0, BLK + 32), :]
            acc = jnp.zeros((BLK, 128), F32)
            for r in range(8):
                turned = v if r == 0 else pltpu.roll(v, BLK + 32 - r, axis=0)
                for m in range(4):
                    o = 8 * m + r - 1
                    if 0 <= o < TAPS:
                        acc = acc + turned[8 * m : 8 * m + BLK] * taps[o : o + 1]
            acc = acc * mask_own[b]
            conv[cc, pl.ds(r0, BLK), :] = acc
            return total + jnp.sum(acc.reshape(BLK // 8, 8, 128), axis=0)

        total = lax.fori_loop(0, NB, rows, jnp.zeros((8, 128), F32))
        average = jnp.sum(total, axis=0, keepdims=True) * (1.0 / PAIR)

        def deviations(b, total):
            r0 = pl.multiple_of(b * BLK, BLK)
            diff = (conv[cc, pl.ds(r0, BLK), :] - average) * mask_own[b]
            return total + jnp.sum((diff * diff).reshape(BLK // 8, 8, 128), axis=0)

        square = lax.fori_loop(0, NB, deviations, jnp.zeros((8, 128), F32))
        st_own[0, j] = average
        st_own[1, j] = jnp.sum(square, axis=0, keepdims=True)
        at = pl.ds(pl.multiple_of((1 - c) * BLK, BLK), PAIR)
        pltpu.make_async_remote_copy(
            src_ref=conv.at[cc, at], dst_ref=conv.at[cc, at], send_sem=c_send, recv_sem=c_recv,
            device_id=mate, device_id_type=MESH,
        ).start()

    def natural(j):
        for g in range(4):
            part = weights[pl.ds((N_IN + j) * 16 + g * 4, 4)].reshape(384, 256)
            w_nat[c, j, g * 384 : (g + 1) * 384, :] = jnp.dot(
                order_ref[...], part, preferred_element_type=F32
            ).astype(BF16)
        pltpu.make_async_remote_copy(
            src_ref=w_nat.at[c, j], dst_ref=w_nat.at[c, j], send_sem=w_send, recv_sem=w_recv,
            device_id=mate, device_id_type=MESH,
        ).start()

    def loop(lo, hi, f):
        lax.fori_loop(lo, hi, lambda k, carry: (f(k), carry)[1], 0)

    gated[0:16, :] = jnp.zeros((16, 128), F32)
    gated[ROWS + 16 : ROWS + 32, :] = jnp.zeros((16, 128), F32)

    loop(0, NCH, z_start)
    normed_own[8 * (1 - c)] = jnp.zeros((BLK, D), BF16)
    mask_own[8 * (1 - c)] = jnp.zeros((BLK, 128), F32)

    e1(0)
    loop(0, 2, layer_norm_block)
    e2(0)
    loop(2, 4, layer_norm_block)
    e1(1)
    e3(0)
    loop(4, 6, layer_norm_block)
    e2(1)
    e4(0)
    loop(6, 8, layer_norm_block)
    masks = pl.ds(c, 8)
    pltpu.make_async_remote_copy(
        src_ref=mask_own.at[masks], dst_ref=mask_mate.at[masks], send_sem=m_send, recv_sem=m_recv,
        device_id=mate, device_id_type=MESH,
    ).start()
    normed_mate[8 * c] = jnp.zeros((BLK, D), BF16)
    mask_mate[8 * c] = jnp.zeros((BLK, 128), F32)
    wait_for(normed_mate.at[pl.ds(0, 8)], n_send)
    wait_for(mask_mate.at[pl.ds(0, 8)], m_send)
    wait_for(normed_mate.at[pl.ds(0, 8)], n_recv)
    wait_for(mask_mate.at[pl.ds(0, 8)], m_recv)

    def join(q):
        normed_own[q] = normed_own[q] + normed_mate[q]
        mask_own[q] = mask_own[q] + mask_mate[q]

    loop(0, NB, join)

    def slot(m):
        pl.when(m < NCH)(lambda: e1(m))
        pl.when(m < NCH + 1)(lambda: e3(m - 1))
        e5(m - 2)
        pl.when(m - 2 < N_IN)(lambda: project(m - 2))
        pl.when(m - 2 >= N_IN)(lambda: natural(m - 2 - N_IN))
        pl.when(m < NCH)(lambda: e2(m))
        pl.when(m < NCH + 1)(lambda: e4(m - 1))
        pl.when(m - 2 < N_IN)(lambda: convolve(m - 2))

    loop(2, N_IN + 2, slot)

    me_a = x * 4 + y
    st_a[me_a] = st_own[...]

    def send_a(k):
        xx, yy = xy_peer(k)
        pltpu.make_async_remote_copy(
            src_ref=st_own, dst_ref=st_a.at[me_a], send_sem=sa_send, recv_sem=sa_recv,
            device_id=device(xx, yy, z, c), device_id_type=MESH,
        ).start()

    loop(1, 16, send_a)
    slot(N_IN + 2)
    wait_for(st_a.at[pl.ds(0, 15)], sa_recv)
    all_a = st_a[...]
    mean_a = jnp.sum(all_a[:, 0], axis=0) * (1.0 / 16)
    off_a = all_a[:, 0] - mean_a[None]
    st_b0[0] = mean_a
    st_b0[1] = jnp.sum(all_a[:, 1], axis=0) + PAIR * jnp.sum(off_a * off_a, axis=0)
    me_b = c * 8 + z
    st_b[me_b] = st_b0[...]

    def send_b(k):
        zz, cc = z_peer(k)
        pltpu.make_async_remote_copy(
            src_ref=st_b0, dst_ref=st_b.at[me_b], send_sem=sb_send, recv_sem=sb_recv,
            device_id=device(x, y, zz, cc), device_id_type=MESH,
        ).start()

    loop(1, 16, send_b)
    slot(N_IN + 3)
    slot(N_IN + 4)
    wait_for(st_b.at[pl.ds(0, 15)], sb_recv)
    for h in range(2):
        part = st_b[h * 8 : h * 8 + 8]
        mean_b = jnp.sum(part[:, 0], axis=0) * (1.0 / 8)
        off_b = part[:, 0] - mean_b[None]
        spread = (
            jnp.sum(part[:, 1], axis=0) + (16 * PAIR) * jnp.sum(off_b * off_b, axis=0)
        ) * (1.0 / TOTAL)
        stats[0, h * 6 : h * 6 + 6] = mean_b
        stats[1, h * 6 : h * 6 + 6] = lax.rsqrt(spread + EPSILON)

    at_mine = pl.ds(pl.multiple_of(c * BLK, BLK), PAIR)
    wait_for(conv.at[pl.ds(0, 6), pl.ds(0, PAIR)], c_recv)
    wait_for(w_nat.at[0], w_recv)

    def activate(qi):
        q = qi + c
        at = pl.ds(pl.multiple_of(q * BLK, BLK), BLK)
        for cc in range(12):
            lanes = slice(cc * 128, cc * 128 + 128)
            v = conv[cc, at, :] - stats[0, cc]
            v = v * (stats[1, cc] * bgain_ref[:, lanes]) + bbias_ref[:, lanes]
            act[pl.ds(q * 8, 8), :, lanes] = jax.nn.silu(v).astype(BF16).reshape(8, 16, 128)

    loop(0, 8, activate)

    def finish(t):
        i0 = t * BLK
        low = base + i0
        w = jnp.minimum(lax.div(low, 16), (ROWS - WIN) // 16)
        i = i0 + lax.broadcasted_iota(jnp.int32, (BLK, WIN), 0)
        r = w * 16 + lax.broadcasted_iota(jnp.int32, (BLK, WIN), 1)
        chosen = jnp.logical_and(place(i) == r, i < n_own).astype(F32).astype(BF16)
        mine = jnp.dot(chosen, window(act, w), preferred_element_type=F32).astype(BF16)
        rows = pl.ds(t * 8, 8)
        live = i0 + lax.broadcasted_iota(jnp.int32, (BLK, 256), 0) < n_own
        for h in range(2):
            for k in range(N_OUT):
                lo = h * HALF + k * 256
                branch = jnp.dot(mine, w_nat[h, k], preferred_element_type=F32)
                res = x_ref[rows, :, lo : lo + 256].reshape(BLK, 256).astype(F32) + branch
                out_ref[rows, :, lo : lo + 256] = jnp.where(live, res, 0.0).astype(BF16).reshape(8, 16, 256)

    loop(0, CAP // BLK, finish)

    wait_for(zin.at[:, pl.ds(0, 15)], z_send)
    wait_for(weights.at[pl.ds(0, 135)], ring_send)
    wait_for(conv.at[pl.ds(0, 6), pl.ds(0, PAIR)], c_send)
    wait_for(w_nat.at[0], w_send)
    wait_for(st_a.at[pl.ds(0, 15)], sa_send)
    wait_for(st_b.at[pl.ds(0, 15)], sb_send)


def on_device(
    frames_in, lengths, norm_gain, norm_bias, w_in, taps, batch_gain, batch_bias, w_out
):
    vmem = pl.BlockSpec(memory_space=pltpu.VMEM)
    dma = pltpu.SemaphoreType.DMA
    out = pl.pallas_call(
        kernel,
        out_shape=jax.ShapeDtypeStruct((CAP // 16, 16, D), BF16),
        in_specs=[pl.BlockSpec(memory_space=pltpu.SMEM)] + [vmem] * 10,
        out_specs=vmem,
        scratch_shapes=[
            pltpu.VMEM((2, NCH, 8, 256), BF16),
            pltpu.VMEM((NCH, 16, 8, 256), BF16),
            pltpu.VMEM((NCH * 16, 96, 256), BF16),
            pltpu.VMEM((BLK, D), F32),
            pltpu.VMEM((NB, BLK, D), BF16),
            pltpu.VMEM((NB, BLK, D), BF16),
            pltpu.VMEM((NB, BLK, 128), F32),
            pltpu.VMEM((NB, BLK, 128), F32),
            pltpu.VMEM((3 * BLK, 256), F32),
            pltpu.VMEM((ROWS + 32, 128), F32),
            pltpu.VMEM((12, ROWS, 128), F32),
            pltpu.VMEM((ROWS // 16, 16, D), BF16),
            pltpu.VMEM((2, N_OUT, D, 256), BF16),
            pltpu.VMEM((2, 6, 1, 128), F32),
            pltpu.VMEM((16, 2, 6, 1, 128), F32),
            pltpu.VMEM((2, 6, 1, 128), F32),
            pltpu.VMEM((16, 2, 6, 1, 128), F32),
            pltpu.VMEM((2, 12, 1, 128), F32),
            dma, dma((NCH,)), dma, dma((NCH, 3)), dma((NCH, 3)),
            dma, dma, dma, dma, dma, dma, dma, dma, dma, dma, dma, dma,
        ],
        compiler_params=pltpu.CompilerParams(
            collective_id=0, has_side_effects=True, vmem_limit_bytes=60 * 2**20
        ),
        cost_estimate=pl.CostEstimate(
            flops=20 * 10**9, bytes_accessed=10**7, transcendentals=4 * 10**6
        ),
    )(
        lengths.reshape(4), frames_in.reshape(CAP // 16, 16, D), norm_gain.reshape(1, D), norm_bias.reshape(1, D),
        w_in, w_out, taps, batch_gain.reshape(1, D), batch_bias.reshape(1, D),
        jnp.asarray(feature_order(), BF16), jnp.asarray(compaction(), BF16),
    )
    return out.reshape(1, CAP, D)


def solution(mesh):
    placed = (
        P("rep", "dp", None), P("rep", "dp", None), P(), P(), P(("dp", "rep"), None),
        P(), P(), P(), P(("dp", "rep"), None),
    )
    return jax.shard_map(
        on_device, mesh=mesh, in_specs=placed, out_specs=P("rep", "dp", None), check_vma=False
    )
```

```python
import functools

import jax
import jax.numpy as jnp
import numpy as np
from jax import lax
from jax.experimental import pallas as pl
from jax.experimental.pallas import tpu as pltpu
from jax.sharding import PartitionSpec as P

EPSILON = 1e-05
MESH = pl.DeviceIdType.MESH
F32 = jnp.float32
BF16 = jnp.bfloat16

NX, NY, NZ, NC = 4, 4, 8, 2
D = 1536
HALF = D // 2
CAP = 896
PAIR = 1024
GAP = 15
ROWS = 1152
BLK = 128
NB = ROWS // BLK
WIN = 192
TAPS = 31
N_IN = 6
TOTAL = 512 * 256


def feature_order():
    order = np.zeros((384, 384), np.float32)
    for z in range(8):
        for c in range(2):
            for y in range(4):
                for i in range(6):
                    order[z * 48 + c * 24 + y * 6 + i, y * 96 + z * 12 + c * 6 + i] = 1.0
    return order


def compaction():
    pick = np.zeros((96, 128), np.float32)
    for k in range(16):
        for i in range(6):
            pick[k * 6 + i, k * 8 + i] = 1.0
    return pick


def kernel(
    lengths_ref, x_ref, gain_ref, bias_ref, w_in_ref, w_out_ref, taps_ref, bgain_ref, bbias_ref,
    order_ref, pick_ref,
    out_ref,
    slab, slab_o, zin, zin_o, weights, wout, xs, normed_own, normed_mate, mask_own, mask_mate,
    proj, gated, conv, act, w_nat, st_own, st_a, st_b0, st_b, stats,
    z_send, zo_send, z_recv, r1_send, r2_send, r3_send, r1_recv, r2_recv, r3_recv, n_send, n_recv, m_send, m_recv,
    c_send, c_recv, w_send, w_recv, sa_send, sa_recv, sb_send, sb_recv,
):
    dp = lax.axis_index("dp")
    y = lax.axis_index("rep")
    x = dp // 16
    z = lax.rem(dp // 2, 8)
    c = lax.rem(dp, 2)
    flips = [(1 - 2 * lax.rem(dp // 2**b, 2)) * 2**b for b in range(6)]
    y_flips = [(1 - 2 * lax.rem(y // 2**b, 2)) * 2**b for b in range(2)]

    def flip(start, deltas, k):
        for b, delta in enumerate(deltas):
            if k >> b & 1:
                start = start + delta
        return start

    mate = (flip(dp, flips, 1), y)
    z_peers = [(flip(dp, flips, k), y) for k in range(16)]
    xy_peers = [(flip(dp, flips, (k >> 2) << 4), flip(y, y_flips, k & 3)) for k in range(16)]
    xs_at = [lax.rem(x + k, 4) for k in range(4)]
    ys_at = [lax.rem(y + k, 4) for k in range(4)]
    me_z = z * 2 + c
    me_xy = x * 4 + y

    barrier = pltpu.get_barrier_semaphore()
    for k in range(1, 16):
        pl.semaphore_signal(barrier, 1, device_id=z_peers[k], device_id_type=MESH)
        pl.semaphore_signal(barrier, 1, device_id=xy_peers[k], device_id_type=MESH)

    slab[...] = jnp.zeros_like(slab)
    slab_o[...] = jnp.zeros_like(slab_o)
    for h in range(2):
        for j in range(N_IN):
            lo = h * HALF + j * 128
            slab[h, j // 2, j % 2, 0:6, 0:128] = w_in_ref[:, lo : lo + 128]
            slab[h, j // 2, j % 2, 0:6, 128:256] = w_in_ref[:, D + lo : D + lo + 128]
        for j in range(2):
            lo = h * HALF + j * 384
            slab_o[h, j, 0:6, :] = w_out_ref[:, lo : lo + 384]
    for p in range(3):
        zin[p, me_z] = slab[c, p]
    zin_o[me_z] = slab_o[c]

    pl.semaphore_wait(barrier, 30)

    def send(src, dst, sent, landed, to):
        pltpu.make_async_remote_copy(
            src_ref=src, dst_ref=dst, send_sem=sent, recv_sem=landed,
            device_id=to, device_id_type=MESH,
        ).start()

    def wait_for(ref, sem):
        pltpu.make_async_copy(ref, ref, sem).wait()

    def s0(p):
        for k in range(1, 16):
            other = 1 - c if k % 2 else c
            if p < 3:
                send(slab.at[other, p], zin.at[p, me_z], z_send, z_recv.at[p], z_peers[k])
            else:
                send(slab_o.at[other], zin_o.at[me_z], zo_send, z_recv.at[p], z_peers[k])

    def chunk(p, a):
        return weights.at[2 * p + a] if p < 3 else wout.at[a]

    def kind(p):
        return 0 if p < 3 else 1

    def for_core(f):
        pl.when(c == 0)(lambda: f(0))
        pl.when(c == 1)(lambda: f(1))

    def s1(p):
        if p < 3:
            wait_for(zin.at[0, pl.ds(0, 15)], z_recv.at[p])
        else:
            wait_for(zin_o.at[pl.ds(0, 15)], z_recv.at[p])
        for a in range(2):
            rows = (zin[p, :, a] if p < 3 else zin_o[:, a]).reshape(128, 256 if p < 3 else 384)
            chunk(p, a)[x, y] = jnp.dot(
                pick_ref[...], rows, preferred_element_type=F32
            ).astype(BF16)

        def go(v):
            for a in range(2):
                ref = chunk(p, a).at[x, y]
                for k in (1, 3, 2):
                    to = (dp + (xs_at[k] - x) * 16, y) if (v + a) % 2 == 0 else (dp, ys_at[k])
                    send(ref, ref, r1_send.at[kind(p)], r1_recv.at[p], to)

        for_core(go)

    def second(p, a, v, origin, part):
        if (v + a) % 2 == 0:
            return chunk(p, a).at[part, ys_at[origin]]
        return chunk(p, a).at[xs_at[origin], part]

    def second_to(a, v, k):
        return (dp, ys_at[k]) if (v + a) % 2 == 0 else (dp + (xs_at[k] - x) * 16, y)

    def s2(p):
        wait_for(chunk(p, 0).at[pl.ds(0, 2), pl.ds(0, 3)], r1_recv.at[p])

        def go(v):
            for a in range(2):
                ref = second(p, a, v, 0, pl.ds(0, 4))
                for k in (1, 3):
                    send(ref, ref, r2_send.at[kind(p)], r2_recv.at[p], second_to(a, v, k))

        for_core(go)

    def s3(p):
        wait_for(chunk(p, 0), r2_recv.at[p])

        def go(v):
            for a in range(2):
                for k, part in ((1, pl.ds(0, 2)), (3, pl.ds(2, 2))):
                    ref = second(p, a, v, 4 - k, part)
                    send(ref, ref, r3_send.at[kind(p)], r3_recv.at[p], second_to(a, v, k))

        for_core(go)

    def s4(p):
        wait_for(chunk(p, 0).at[pl.ds(0, 2)], r3_recv.at[p])

    n_own = lengths_ref[0] + lengths_ref[1] + lengths_ref[2] + lengths_ref[3]
    b0 = lengths_ref[0]
    b1 = b0 + lengths_ref[1]
    b2 = b1 + lengths_ref[2]
    base = c * (PAIR - n_own + 4 * GAP)

    def place(i):
        u = (i >= b0).astype(jnp.int32) + (i >= b1).astype(jnp.int32) + (i >= b2).astype(jnp.int32)
        return i + base + GAP * u

    def window(ref, w):
        return jnp.concatenate([ref[w + k] for k in range(WIN // 16)], axis=0)

    def layer_norm_block(qi):
        q = qi + c
        low = jnp.maximum(q * BLK - base - 3 * GAP, 0)
        w = jnp.minimum(lax.div(low, 16), (CAP - WIN) // 16)
        i = w * 16 + lax.broadcasted_iota(jnp.int32, (BLK, WIN), 1)
        r = q * BLK + lax.broadcasted_iota(jnp.int32, (BLK, WIN), 0)
        chosen = jnp.logical_and(place(i) == r, i < n_own).astype(F32)
        xs[...] = jnp.dot(chosen.astype(BF16), window(x_ref, w), preferred_element_type=F32)
        live = jnp.broadcast_to(jnp.sum(chosen, axis=1, keepdims=True), (BLK, 128))
        mask_own[q] = live

        def rows(g, carry):
            at = pl.ds(pl.multiple_of(g * 16, 16), 16)
            v = xs[at, :]
            average = jnp.sum(v, axis=1, keepdims=True) * (1.0 / D)
            centred = v - average
            spread = jnp.sum(centred * centred, axis=1, keepdims=True) * (1.0 / D)
            res = centred * lax.rsqrt(spread + EPSILON) * gain_ref[...] + bias_ref[...]
            m = mask_own[q, at, 0:1]
            normed_own[q, at, :] = jnp.where(m > 0.0, res, 0.0).astype(BF16)
            return carry

        lax.fori_loop(0, BLK // 16, rows, 0)
        for g in range(4):
            cols = slice(g * 384, (g + 1) * 384)
            normed_own[q, :, cols] = jnp.dot(
                normed_own[q, :, cols], order_ref[...], preferred_element_type=F32
            ).astype(BF16)
        pltpu.make_async_remote_copy(
            src_ref=normed_own.at[q], dst_ref=normed_mate.at[q], send_sem=n_send, recv_sem=n_recv,
            device_id=mate, device_id_type=MESH,
        ).start()

    def project(j):
        w = weights[j].reshape(D, 256)

        def rows(b, carry):
            at = pl.ds(b * 3, 3)
            proj[...] = jnp.dot(
                normed_own[at].reshape(3 * BLK, D), w, preferred_element_type=F32
            )
            v = proj[:, 0:128]
            g = proj[:, 128:256]
            res = v * jax.nn.sigmoid(g)
            gated[pl.ds(pl.multiple_of(16 + b * 3 * BLK, 16), 3 * BLK), :] = res.astype(BF16).astype(F32)
            return carry

        lax.fori_loop(0, NB // 3, rows, 0)

    def convolve(j):
        cc = c * N_IN + j
        lanes = pl.ds(pl.multiple_of(cc * 128, 128), 128)
        taps = taps_ref[:, lanes]

        def rows(b, total):
            r0 = pl.multiple_of(b * BLK, BLK)
            v = gated[pl.ds(r0, BLK + 32), :]
            acc = jnp.zeros((BLK, 128), F32)
            for r in range(8):
                turned = v if r == 0 else pltpu.roll(v, BLK + 32 - r, axis=0)
                for m in range(4):
                    o = 8 * m + r - 1
                    if 0 <= o < TAPS:
                        acc = acc + turned[8 * m : 8 * m + BLK] * taps[o : o + 1]
            acc = acc * mask_own[b]
            conv[cc, pl.ds(r0, BLK), :] = acc
            return total + jnp.sum(acc.reshape(BLK // 8, 8, 128), axis=0)

        total = lax.fori_loop(0, NB, rows, jnp.zeros((8, 128), F32))
        average = jnp.sum(total, axis=0, keepdims=True) * (1.0 / PAIR)

        def deviations(b, total):
            r0 = pl.multiple_of(b * BLK, BLK)
            diff = (conv[cc, pl.ds(r0, BLK), :] - average) * mask_own[b]
            return total + jnp.sum((diff * diff).reshape(BLK // 8, 8, 128), axis=0)

        square = lax.fori_loop(0, NB, deviations, jnp.zeros((8, 128), F32))
        st_own[0, j] = average
        st_own[1, j] = jnp.sum(square, axis=0, keepdims=True)
        at = pl.ds(pl.multiple_of((1 - c) * BLK, BLK), PAIR)
        pltpu.make_async_remote_copy(
            src_ref=conv.at[cc, at], dst_ref=conv.at[cc, at], send_sem=c_send, recv_sem=c_recv,
            device_id=mate, device_id_type=MESH,
        ).start()

    def natural(a):
        for g in range(4):
            w_nat[c, a, g * 384 : (g + 1) * 384, :] = jnp.dot(
                order_ref[...], wout[a, g].reshape(384, 384), preferred_element_type=F32
            ).astype(BF16)
        send(w_nat.at[c, a], w_nat.at[c, a], w_send, w_recv, mate)

    def loop(lo, hi, f):
        lax.fori_loop(lo, hi, lambda k, carry: (f(k), carry)[1], 0)

    gated[0:16, :] = jnp.zeros((16, 128), F32)
    gated[ROWS + 16 : ROWS + 32, :] = jnp.zeros((16, 128), F32)

    s0(0)
    s0(1)
    normed_own[8 * (1 - c)] = jnp.zeros((BLK, D), BF16)
    mask_own[8 * (1 - c)] = jnp.zeros((BLK, 128), F32)
    normed_mate[8 * c] = jnp.zeros((BLK, D), BF16)
    mask_mate[8 * c] = jnp.zeros((BLK, 128), F32)

    def norm_step(i):
        layer_norm_block(i)

        @pl.when(i == 1)
        def _():
            s1(0)
            s0(2)

        @pl.when(i == 2)
        def _():
            s1(1)
            s0(3)

        @pl.when(i == 3)
        def _():
            s2(0)

        @pl.when(i == 4)
        def _():
            s2(1)
            s1(2)

        @pl.when(i == 6)
        def _():
            s1(3)

    loop(0, 8, norm_step)
    masks = pl.ds(c, 8)
    send(mask_own.at[masks], mask_mate.at[masks], m_send, m_recv, mate)
    s3(0)
    s2(2)
    wait_for(normed_mate.at[pl.ds(0, 8)], n_send)
    wait_for(mask_mate.at[pl.ds(0, 8)], m_send)
    wait_for(normed_mate.at[pl.ds(0, 8)], n_recv)
    wait_for(mask_mate.at[pl.ds(0, 8)], m_recv)

    def join(q):
        normed_own[q] = normed_own[q] + normed_mate[q]
        mask_own[q] = mask_own[q] + mask_mate[q]

    loop(0, NB, join)
    s3(1)
    s2(3)
    s4(0)

    def compute(j):
        project(j)

        @pl.when(j == 1)
        def _():
            s3(2)

        convolve(j)

        @pl.when(j == 1)
        def _():
            s4(1)

        @pl.when(j == 2)
        def _():
            s3(3)

        @pl.when(j == 3)
        def _():
            s4(2)

    loop(0, N_IN, compute)

    st_a[me_xy] = st_own[...]
    for k in range(1, 16):
        send(st_own, st_a.at[me_xy], sa_send, sa_recv, xy_peers[k])
    s4(3)
    natural(0)
    natural(1)
    wait_for(st_a.at[pl.ds(0, 15)], sa_recv)
    all_a = st_a[...]
    mean_a = jnp.sum(all_a[:, 0], axis=0) * (1.0 / 16)
    off_a = all_a[:, 0] - mean_a[None]
    st_b0[0] = mean_a
    st_b0[1] = jnp.sum(all_a[:, 1], axis=0) + PAIR * jnp.sum(off_a * off_a, axis=0)
    me_b = c * 8 + z
    st_b[me_b] = st_b0[...]
    for k in range(1, 16):
        send(st_b0, st_b.at[me_b], sb_send, sb_recv, z_peers[k])
    wait_for(st_b.at[pl.ds(0, 15)], sb_recv)
    for h in range(2):
        part = st_b[h * 8 : h * 8 + 8]
        mean_b = jnp.sum(part[:, 0], axis=0) * (1.0 / 8)
        off_b = part[:, 0] - mean_b[None]
        spread = (
            jnp.sum(part[:, 1], axis=0) + (16 * PAIR) * jnp.sum(off_b * off_b, axis=0)
        ) * (1.0 / TOTAL)
        stats[0, h * 6 : h * 6 + 6] = mean_b
        stats[1, h * 6 : h * 6 + 6] = lax.rsqrt(spread + EPSILON)

    at_mine = pl.ds(pl.multiple_of(c * BLK, BLK), PAIR)
    wait_for(conv.at[pl.ds(0, 6), pl.ds(0, PAIR)], c_recv)
    wait_for(w_nat.at[0], w_recv)

    def activate(qi):
        q = qi + c
        at = pl.ds(pl.multiple_of(q * BLK, BLK), BLK)
        for cc in range(12):
            lanes = slice(cc * 128, cc * 128 + 128)
            v = conv[cc, at, :] - stats[0, cc]
            v = v * (stats[1, cc] * bgain_ref[:, lanes]) + bbias_ref[:, lanes]
            act[pl.ds(q * 8, 8), :, lanes] = jax.nn.silu(v).astype(BF16).reshape(8, 16, 128)

    loop(0, 8, activate)

    def finish(t):
        i0 = t * BLK
        low = base + i0
        w = jnp.minimum(lax.div(low, 16), (ROWS - WIN) // 16)
        i = i0 + lax.broadcasted_iota(jnp.int32, (BLK, WIN), 0)
        r = w * 16 + lax.broadcasted_iota(jnp.int32, (BLK, WIN), 1)
        chosen = jnp.logical_and(place(i) == r, i < n_own).astype(F32).astype(BF16)
        mine = jnp.dot(chosen, window(act, w), preferred_element_type=F32).astype(BF16)
        rows = pl.ds(t * 8, 8)
        live = i0 + lax.broadcasted_iota(jnp.int32, (BLK, 384), 0) < n_own
        for h in range(2):
            for k in range(2):
                lo = h * HALF + k * 384
                branch = jnp.dot(mine, w_nat[h, k], preferred_element_type=F32)
                res = x_ref[rows, :, lo : lo + 384].reshape(BLK, 384).astype(F32) + branch
                out_ref[rows, :, lo : lo + 384] = jnp.where(live, res, 0.0).astype(BF16).reshape(8, 16, 384)

    loop(0, CAP // BLK, finish)

    wait_for(zin.at[:, pl.ds(0, 15)], z_send)
    wait_for(zin_o.at[pl.ds(0, 15)], zo_send)
    wait_for(weights.at[:, pl.ds(0, 3), 0], r1_send.at[0])
    wait_for(weights.at[pl.ds(0, 3)], r2_send.at[0])
    wait_for(weights.at[:, 0], r3_send.at[0])
    wait_for(wout.at[0, pl.ds(0, 2), pl.ds(0, 3)], r1_send.at[1])
    wait_for(wout.at[0], r2_send.at[1])
    wait_for(wout.at[0, pl.ds(0, 2)], r3_send.at[1])
    wait_for(conv.at[pl.ds(0, 6), pl.ds(0, PAIR)], c_send)
    wait_for(w_nat.at[0], w_send)
    wait_for(st_a.at[pl.ds(0, 15)], sa_send)
    wait_for(st_b.at[pl.ds(0, 15)], sb_send)


def on_device(
    frames_in, lengths, norm_gain, norm_bias, w_in, taps, batch_gain, batch_bias, w_out
):
    vmem = pl.BlockSpec(memory_space=pltpu.VMEM)
    dma = pltpu.SemaphoreType.DMA
    out = pl.pallas_call(
        kernel,
        out_shape=jax.ShapeDtypeStruct((CAP // 16, 16, D), BF16),
        in_specs=[pl.BlockSpec(memory_space=pltpu.SMEM)] + [vmem] * 10,
        out_specs=vmem,
        scratch_shapes=[
            pltpu.VMEM((2, 3, 2, 8, 256), BF16),
            pltpu.VMEM((2, 2, 8, 384), BF16),
            pltpu.VMEM((3, 16, 2, 8, 256), BF16),
            pltpu.VMEM((16, 2, 8, 384), BF16),
            pltpu.VMEM((N_IN, 4, 4, 96, 256), BF16),
            pltpu.VMEM((2, 4, 4, 96, 384), BF16),
            pltpu.VMEM((BLK, D), F32),
            pltpu.VMEM((NB, BLK, D), BF16),
            pltpu.VMEM((NB, BLK, D), BF16),
            pltpu.VMEM((NB, BLK, 128), F32),
            pltpu.VMEM((NB, BLK, 128), F32),
            pltpu.VMEM((3 * BLK, 256), F32),
            pltpu.VMEM((ROWS + 32, 128), F32),
            pltpu.VMEM((12, ROWS, 128), F32),
            pltpu.VMEM((ROWS // 16, 16, D), BF16),
            pltpu.VMEM((2, 2, D, 384), BF16),
            pltpu.VMEM((2, 6, 1, 128), F32),
            pltpu.VMEM((16, 2, 6, 1, 128), F32),
            pltpu.VMEM((2, 6, 1, 128), F32),
            pltpu.VMEM((16, 2, 6, 1, 128), F32),
            pltpu.VMEM((2, 12, 1, 128), F32),
            dma, dma, dma((4,)), dma((2,)), dma((2,)), dma((2,)), dma((4,)), dma((4,)), dma((4,)),
            dma, dma, dma, dma, dma, dma, dma, dma, dma, dma, dma, dma,
        ],
        compiler_params=pltpu.CompilerParams(
            collective_id=0, has_side_effects=True, vmem_limit_bytes=60 * 2**20
        ),
        cost_estimate=pl.CostEstimate(
            flops=20 * 10**9, bytes_accessed=10**7, transcendentals=4 * 10**6
        ),
    )(
        lengths.reshape(4), frames_in.reshape(CAP // 16, 16, D), norm_gain.reshape(1, D), norm_bias.reshape(1, D),
        w_in, w_out, taps, batch_gain.reshape(1, D), batch_bias.reshape(1, D),
        jnp.asarray(feature_order(), BF16), jnp.asarray(compaction(), BF16),
    )
    return out.reshape(1, CAP, D)


def solution(mesh):
    placed = (
        P("rep", "dp", None), P("rep", "dp", None), P(), P(), P(("dp", "rep"), None),
        P(), P(), P(), P(("dp", "rep"), None),
    )
    return jax.shard_map(
        on_device, mesh=mesh, in_specs=placed, out_specs=P("rep", "dp", None), check_vma=False
    )
```

```python
import functools

import jax
import jax.numpy as jnp
import numpy as np
from jax import lax
from jax.experimental import pallas as pl
from jax.experimental.pallas import tpu as pltpu
from jax.sharding import PartitionSpec as P

EPSILON = 1e-05
MESH = pl.DeviceIdType.MESH
F32 = jnp.float32
BF16 = jnp.bfloat16

NX, NY, NZ, NC = 4, 4, 8, 2
D = 1536
HALF = D // 2
CAP = 896
PAIR = 1024
GAP = 15
ROWS = 1152
BLK = 128
NB = ROWS // BLK
WIN = 192
TAPS = 31
N_IN = 6
TOTAL = 512 * 256


def feature_order():
    order = np.zeros((384, 384), np.float32)
    for z in range(8):
        for c in range(2):
            for y in range(4):
                for i in range(6):
                    order[z * 48 + c * 24 + y * 6 + i, y * 96 + z * 12 + c * 6 + i] = 1.0
    return order


def compaction():
    pick = np.zeros((96, 128), np.float32)
    for k in range(16):
        for i in range(6):
            pick[k * 6 + i, k * 8 + i] = 1.0
    return pick


def kernel(
    lengths_ref, x_ref, gain_1d, bias_1d, w_in_ref, w_out_ref, taps_ref, bgain_1d, bbias_1d,
    order_ref, pick_ref,
    out_ref,
    gain_ref, bias_ref, bgain_ref, bbias_ref, slab, slab_o, zin, both_o, zin_o, weights, wout, xs, normed_own, normed_mate, mask_own, mask_mate,
    proj, gated, conv, act, st_own, st_a, st_b0, st_b, stats,
    bo_send, bo_recv, z_send, zo_send, z_recv, zo_recv, r1_send, r2_send, r3_send, r1_recv, r2_recv, r3_recv,
    o_send, o_recv, n_send, n_recv, m_send, m_recv,
    c_send, c_recv, w_send, w_recv, sa_send, sa_recv, sb_send, sb_recv,
):
    dp = lax.axis_index("dp")
    y = lax.axis_index("rep")
    x = dp // 16
    z = lax.rem(dp // 2, 8)
    c = lax.rem(dp, 2)
    flips = [(1 - 2 * lax.rem(dp // 2**b, 2)) * 2**b for b in range(6)]
    y_flips = [(1 - 2 * lax.rem(y // 2**b, 2)) * 2**b for b in range(2)]

    def flip(start, deltas, k):
        for b, delta in enumerate(deltas):
            if k >> b & 1:
                start = start + delta
        return start

    mate = (flip(dp, flips, 1), y)
    z_peers = [(flip(dp, flips, k), y) for k in range(16)]
    xy_peers = [(flip(dp, flips, (k >> 2) << 4), flip(y, y_flips, k & 3)) for k in range(16)]
    zs_at = [lax.rem(z + k, 8) for k in range(8)]
    xs_at = [lax.rem(x + k, 4) for k in range(4)]
    ys_at = [lax.rem(y + k, 4) for k in range(4)]
    me_z = z * 2 + c
    me_xy = x * 4 + y

    barrier = pltpu.get_barrier_semaphore()
    for k in range(1, 16):
        pl.semaphore_signal(barrier, 1, device_id=z_peers[k], device_id_type=MESH)
        pl.semaphore_signal(barrier, 1, device_id=xy_peers[k], device_id_type=MESH)

    for vector, ref in (
        (gain_1d, gain_ref), (bias_1d, bias_ref), (bgain_1d, bgain_ref), (bbias_1d, bbias_ref)
    ):
        ref[...] = vector[...].reshape(1, D)

    slab[...] = jnp.zeros_like(slab)
    slab_o[...] = jnp.zeros_like(slab_o)
    for h in range(2):
        for j in range(N_IN):
            lo = h * HALF + j * 128
            slab[h, j // 2, j % 2, 0:6, 0:128] = w_in_ref[:, lo : lo + 128]
            slab[h, j // 2, j % 2, 0:6, 128:256] = w_in_ref[:, D + lo : D + lo + 128]
        for j in range(2):
            lo = h * HALF + j * 384
            slab_o[h, j, 0:6, :] = w_out_ref[:, lo : lo + 384]
    for p in range(3):
        zin[me_z, p] = slab[c, p]
    both_o[c] = slab_o[c]

    pl.semaphore_wait(barrier, 30)

    def send(src, dst, sent, landed, to):
        pltpu.make_async_remote_copy(
            src_ref=src, dst_ref=dst, send_sem=sent, recv_sem=landed,
            device_id=to, device_id_type=MESH,
        ).start()

    def wait_for(ref, sem):
        pltpu.make_async_copy(ref, ref, sem).wait()

    def s0(p):
        for k in range(1, 16):
            other = 1 - c if k % 2 else c
            part = pl.ds(p, 1 + p)
            send(slab.at[other, part], zin.at[me_z, part], z_send, z_recv.at[p], z_peers[k])

    def chunk(p, a):
        return weights.at[2 * p + a]

    def for_core(f):
        pl.when(c == 0)(lambda: f(0))
        pl.when(c == 1)(lambda: f(1))

    def s1(p):
        if p < 2:
            wait_for(zin.at[pl.ds(0, 15), pl.ds(0, 1 + p)], z_recv.at[p])
        for a in range(2):
            rows = zin[:, p, a].reshape(128, 256)
            chunk(p, a)[x, y] = jnp.dot(
                pick_ref[...], rows, preferred_element_type=F32
            ).astype(BF16)

        def go(v):
            for a in range(2):
                ref = chunk(p, a).at[x, y]
                for k in (1, 3, 2):
                    to = (dp + (xs_at[k] - x) * 16, y) if (v + a) % 2 == 0 else (dp, ys_at[k])
                    send(ref, ref, r1_send, r1_recv.at[p], to)

        for_core(go)

    def second(p, a, v, origin, part):
        if (v + a) % 2 == 0:
            return chunk(p, a).at[part, ys_at[origin]]
        return chunk(p, a).at[xs_at[origin], part]

    def second_to(a, v, k):
        return (dp, ys_at[k]) if (v + a) % 2 == 0 else (dp + (xs_at[k] - x) * 16, y)

    def s2(p):
        wait_for(chunk(p, 0).at[pl.ds(0, 2), pl.ds(0, 3)], r1_recv.at[p])

        def go(v):
            for a in range(2):
                ref = second(p, a, v, 0, pl.ds(0, 4))
                for k in (1, 3):
                    send(ref, ref, r2_send, r2_recv.at[p], second_to(a, v, k))

        for_core(go)

    def s3(p):
        wait_for(chunk(p, 0), r2_recv.at[p])

        def go(v):
            for a in range(2):
                for k, part in ((1, pl.ds(0, 2)), (3, pl.ds(2, 2))):
                    ref = second(p, a, v, 4 - k, part)
                    send(ref, ref, r3_send, r3_recv.at[p], second_to(a, v, k))

        for_core(go)

    def s4(p):
        wait_for(chunk(p, 0).at[pl.ds(0, 2)], r3_recv.at[p])

    def o0():
        wait_for(both_o.at[0], bo_recv)
        zin_o[x, :, y] = both_o[...]
        for k in range(1, 16):
            send(both_o, zin_o.at[x, :, y], zo_send, zo_recv, xy_peers[k])

    def bundle(a, k, part=pl.ds(0, 4)):
        return wout.at[c, a, part, zs_at[k]]

    def around(a, t, k, to, part=pl.ds(0, 4)):
        ref = bundle(a, k, part)
        send(ref, ref, o_send.at[0 if t < 3 else 1], o_recv.at[a, t], (dp + (zs_at[to] - z) * 2, y))

    def to_mate(a, k):
        send(bundle(a, k), bundle(a, k), w_send, w_recv, mate)

    def o1():
        wait_for(zin.at[pl.ds(0, 15)], zo_recv)
        for a in range(2):
            for g in range(2):
                rows = zin_o[2 * g : 2 * g + 2, :, :, a].reshape(128, 384)
                block = jnp.dot(pick_ref[...], rows, preferred_element_type=F32).astype(BF16)
                wout[c, a, 2 * g, z] = block[:48]
                wout[c, a, 2 * g + 1, z] = block[48:]
            around(a, 0, 0, 1)
            around(a, 0, 0, 7)
            to_mate(a, 0)

    def o2(t, a):
        wait_for(wout.at[0, a, :, pl.ds(0, 2)], o_recv.at[a, t - 1])
        if t < 3:
            around(a, t, 8 - t, 1)
            around(a, t, t, 7)
        else:
            around(a, t, 5, 1, pl.ds(0, 2))
            around(a, t, 3, 7, pl.ds(2, 2))
        to_mate(a, t)
        to_mate(a, 8 - t)

    def o3(a):
        wait_for(wout.at[0, a, :, 0], o_recv.at[a, 3])
        to_mate(a, 4)

    n_own = lengths_ref[0] + lengths_ref[1] + lengths_ref[2] + lengths_ref[3]
    b0 = lengths_ref[0]
    b1 = b0 + lengths_ref[1]
    b2 = b1 + lengths_ref[2]
    base = c * (PAIR - n_own + 4 * GAP)

    def place(i):
        u = (i >= b0).astype(jnp.int32) + (i >= b1).astype(jnp.int32) + (i >= b2).astype(jnp.int32)
        return i + base + GAP * u

    def window(ref, w):
        return jnp.concatenate([ref[w + k] for k in range(WIN // 16)], axis=0)

    def layer_norm_block(qi):
        q = qi + c
        low = jnp.maximum(q * BLK - base - 3 * GAP, 0)
        w = jnp.minimum(lax.div(low, 16), (CAP - WIN) // 16)
        i = w * 16 + lax.broadcasted_iota(jnp.int32, (BLK, WIN), 1)
        r = q * BLK + lax.broadcasted_iota(jnp.int32, (BLK, WIN), 0)
        chosen = jnp.logical_and(place(i) == r, i < n_own).astype(F32)
        xs[...] = jnp.dot(chosen.astype(BF16), window(x_ref, w), preferred_element_type=F32)
        live = jnp.broadcast_to(jnp.sum(chosen, axis=1, keepdims=True), (BLK, 128))
        mask_own[q] = live

        def rows(g, carry):
            at = pl.ds(pl.multiple_of(g * 16, 16), 16)
            v = xs[at, :]
            average = jnp.sum(v, axis=1, keepdims=True) * (1.0 / D)
            centred = v - average
            spread = jnp.sum(centred * centred, axis=1, keepdims=True) * (1.0 / D)
            res = centred * lax.rsqrt(spread + EPSILON) * gain_ref[...] + bias_ref[...]
            m = mask_own[q, at, 0:1]
            normed_own[q, at, :] = jnp.where(m > 0.0, res, 0.0).astype(BF16)
            return carry

        lax.fori_loop(0, BLK // 16, rows, 0, unroll=4)
        pltpu.make_async_remote_copy(
            src_ref=normed_own.at[q], dst_ref=normed_mate.at[q], send_sem=n_send, recv_sem=n_recv,
            device_id=mate, device_id_type=MESH,
        ).start()

    def project(j):
        w = weights[j].reshape(D, 256)

        def rows(b, carry):
            at = pl.ds(b * 3, 3)
            proj[...] = jnp.dot(
                normed_own[at].reshape(3 * BLK, D), w, preferred_element_type=F32
            )
            v = proj[:, 0:128]
            g = proj[:, 128:256]
            res = v * jax.nn.sigmoid(g)
            gated[pl.ds(pl.multiple_of(16 + b * 3 * BLK, 16), 3 * BLK), :] = res.astype(BF16).astype(F32)
            return carry

        lax.fori_loop(0, NB // 3, rows, 0)

    def convolve(j):
        cc = c * N_IN + j
        lanes = pl.ds(pl.multiple_of(cc * 128, 128), 128)
        taps = taps_ref[:, lanes]

        def rows(b, total):
            r0 = pl.multiple_of(b * BLK, BLK)
            v = gated[pl.ds(r0, BLK + 32), :]
            acc = jnp.zeros((BLK, 128), F32)
            for r in range(8):
                turned = v if r == 0 else pltpu.roll(v, BLK + 32 - r, axis=0)
                for m in range(4):
                    o = 8 * m + r - 1
                    if 0 <= o < TAPS:
                        acc = acc + turned[8 * m : 8 * m + BLK] * taps[o : o + 1]
            acc = acc * mask_own[b]
            conv[cc, pl.ds(r0, BLK), :] = acc
            return total + jnp.sum(acc.reshape(BLK // 8, 8, 128), axis=0)

        total = lax.fori_loop(0, NB, rows, jnp.zeros((8, 128), F32))
        average = jnp.sum(total, axis=0, keepdims=True) * (1.0 / PAIR)

        def deviations(b, total):
            r0 = pl.multiple_of(b * BLK, BLK)
            diff = (conv[cc, pl.ds(r0, BLK), :] - average) * mask_own[b]
            return total + jnp.sum((diff * diff).reshape(BLK // 8, 8, 128), axis=0)

        square = lax.fori_loop(0, NB, deviations, jnp.zeros((8, 128), F32))
        st_own[0, j] = average
        st_own[1, j] = jnp.sum(square, axis=0, keepdims=True)
        at = pl.ds(pl.multiple_of((1 - c) * BLK, BLK), PAIR)
        pltpu.make_async_remote_copy(
            src_ref=conv.at[cc, at], dst_ref=conv.at[cc, at], send_sem=c_send, recv_sem=c_recv,
            device_id=mate, device_id_type=MESH,
        ).start()

    def loop(lo, hi, f):
        lax.fori_loop(lo, hi, lambda k, carry: (f(k), carry)[1], 0)

    gated[0:16, :] = jnp.zeros((16, 128), F32)
    gated[ROWS + 16 : ROWS + 32, :] = jnp.zeros((16, 128), F32)

    send(slab_o.at[1 - c], both_o.at[c], bo_send, bo_recv, mate)
    s0(0)
    s0(1)
    normed_own[8 * (1 - c)] = jnp.zeros((BLK, D), BF16)
    mask_own[8 * (1 - c)] = jnp.zeros((BLK, 128), F32)
    normed_mate[8 * c] = jnp.zeros((BLK, D), BF16)
    mask_mate[8 * c] = jnp.zeros((BLK, 128), F32)

    def norm_step(i):
        layer_norm_block(i)

        for at, steps in (
            (0, (o0,)),
            (2, (lambda: s1(0),)),
            (6, (lambda: s2(0), lambda: s1(1))),
        ):
            @pl.when(i == at)
            def _(steps=steps):
                for step in steps:
                    step()

    loop(0, 8, norm_step)
    masks = pl.ds(c, 8)
    send(mask_own.at[masks], mask_mate.at[masks], m_send, m_recv, mate)
    wait_for(normed_mate.at[pl.ds(0, 8)], n_send)
    wait_for(mask_mate.at[pl.ds(0, 8)], m_send)
    wait_for(normed_mate.at[pl.ds(0, 8)], n_recv)
    wait_for(mask_mate.at[pl.ds(0, 8)], m_recv)

    def join(b):
        at = pl.ds(b * 3, 3)
        both = (normed_own[at] + normed_mate[at]).reshape(3 * BLK, D)
        for g in range(4):
            cols = slice(g * 384, (g + 1) * 384)
            normed_own[at, :, cols] = jnp.dot(
                both[:, cols], order_ref[...], preferred_element_type=F32
            ).astype(BF16).reshape(3, BLK, 384)
        mask_own[at] = mask_own[at] + mask_mate[at]

    def join_step(b):
        join(b)

        @pl.when(b == 0)
        def _():
            o1()

    loop(0, NB // 3, join_step)
    s3(0)
    s2(1)
    s1(2)
    o2(1, 0)
    s4(0)

    def compute(j):
        project(j)
        for at, steps in (
            (0, (lambda: o2(1, 1),)), (1, (lambda: o2(2, 1),)),
            (2, (lambda: s3(2),)), (3, (lambda: o2(3, 1),)), (5, (lambda: o3(1),)),
        ):
            @pl.when(j == at)
            def _(steps=steps):
                for step in steps:
                    step()
        convolve(j)
        for at, steps in (
            (0, (lambda: s3(1), lambda: s2(2), lambda: o2(2, 0))), (1, (lambda: s4(1),)),
            (2, (lambda: o2(3, 0),)), (3, (lambda: s4(2),)), (4, (lambda: o3(0),)),
        ):
            @pl.when(j == at)
            def _(steps=steps):
                for step in steps:
                    step()

    loop(0, N_IN, compute)

    st_a[me_xy] = st_own[...]
    for k in range(1, 16):
        send(st_own, st_a.at[me_xy], sa_send, sa_recv, xy_peers[k])
    wait_for(st_a.at[pl.ds(0, 15)], sa_recv)
    all_a = st_a[...]
    mean_a = jnp.sum(all_a[:, 0], axis=0) * (1.0 / 16)
    off_a = all_a[:, 0] - mean_a[None]
    st_b0[0] = mean_a
    st_b0[1] = jnp.sum(all_a[:, 1], axis=0) + PAIR * jnp.sum(off_a * off_a, axis=0)
    me_b = c * 8 + z
    st_b[me_b] = st_b0[...]
    for k in range(1, 16):
        send(st_b0, st_b.at[me_b], sb_send, sb_recv, z_peers[k])
    wait_for(st_b.at[pl.ds(0, 15)], sb_recv)
    for h in range(2):
        part = st_b[h * 8 : h * 8 + 8]
        mean_b = jnp.sum(part[:, 0], axis=0) * (1.0 / 8)
        off_b = part[:, 0] - mean_b[None]
        spread = (
            jnp.sum(part[:, 1], axis=0) + (16 * PAIR) * jnp.sum(off_b * off_b, axis=0)
        ) * (1.0 / TOTAL)
        stats[0, h * 6 : h * 6 + 6] = mean_b
        stats[1, h * 6 : h * 6 + 6] = lax.rsqrt(spread + EPSILON)

    at_mine = pl.ds(pl.multiple_of(c * BLK, BLK), PAIR)
    wait_for(conv.at[pl.ds(0, 6), pl.ds(0, PAIR)], c_recv)
    wait_for(wout.at[0], w_recv)

    def activate(qi):
        q = qi + c
        at = pl.ds(pl.multiple_of(q * BLK, BLK), BLK)
        for cc in range(12):
            lanes = slice(cc * 128, cc * 128 + 128)
            v = conv[cc, at, :] - stats[0, cc]
            v = v * (stats[1, cc] * bgain_ref[:, lanes]) + bbias_ref[:, lanes]
            act[pl.ds(q * 8, 8), :, lanes] = jax.nn.silu(v).astype(BF16).reshape(8, 16, 128)

    loop(0, 8, activate)

    def finish(t):
        i0 = t * BLK
        low = base + i0
        w = jnp.minimum(lax.div(low, 16), (ROWS - WIN) // 16)
        i = i0 + lax.broadcasted_iota(jnp.int32, (BLK, WIN), 0)
        r = w * 16 + lax.broadcasted_iota(jnp.int32, (BLK, WIN), 1)
        chosen = jnp.logical_and(place(i) == r, i < n_own).astype(F32).astype(BF16)
        mine = jnp.dot(chosen, window(act, w), preferred_element_type=F32).astype(BF16)
        rows = pl.ds(t * 8, 8)
        live = i0 + lax.broadcasted_iota(jnp.int32, (BLK, 384), 0) < n_own
        for h in range(2):
            for k in range(2):
                lo = h * HALF + k * 384
                branch = jnp.dot(
                    mine, wout[h, k].reshape(D, 384), preferred_element_type=F32
                )
                res = x_ref[rows, :, lo : lo + 384].reshape(BLK, 384).astype(F32) + branch
                out_ref[rows, :, lo : lo + 384] = jnp.where(live, res, 0.0).astype(BF16).reshape(8, 16, 384)

    loop(0, CAP // BLK, finish)

    wait_for(zin.at[pl.ds(0, 15)], z_send)
    wait_for(both_o.at[0], bo_send)
    wait_for(zin.at[pl.ds(0, 15)], zo_send)
    wait_for(weights.at[:, pl.ds(0, 3), 0], r1_send)
    wait_for(weights.at[pl.ds(0, 3)], r2_send)
    wait_for(weights.at[:, 0], r3_send)
    wait_for(wout.at[0, :, :, pl.ds(0, 6)], o_send.at[0])
    wait_for(wout.at[0, :, :, 0], o_send.at[1])
    wait_for(conv.at[pl.ds(0, 6), pl.ds(0, PAIR)], c_send)
    wait_for(wout.at[0], w_send)
    wait_for(st_a.at[pl.ds(0, 15)], sa_send)
    wait_for(st_b.at[pl.ds(0, 15)], sb_send)


def on_device(
    frames_in, lengths, norm_gain, norm_bias, w_in, taps, batch_gain, batch_bias, w_out
):
    vmem = pl.BlockSpec(memory_space=pltpu.VMEM)
    dma = pltpu.SemaphoreType.DMA
    out = pl.pallas_call(
        kernel,
        out_shape=jax.ShapeDtypeStruct((CAP // 16, 16, D), BF16),
        in_specs=[pl.BlockSpec(memory_space=pltpu.SMEM)] + [vmem] * 10,
        out_specs=vmem,
        scratch_shapes=[
            pltpu.VMEM((1, D), F32), pltpu.VMEM((1, D), F32),
            pltpu.VMEM((1, D), F32), pltpu.VMEM((1, D), F32),
            pltpu.VMEM((2, 3, 2, 8, 256), BF16),
            pltpu.VMEM((2, 2, 8, 384), BF16),
            pltpu.VMEM((16, 3, 2, 8, 256), BF16),
            pltpu.VMEM((2, 2, 8, 384), BF16),
            pltpu.VMEM((4, 2, 4, 2, 8, 384), BF16),
            pltpu.VMEM((N_IN, 4, 4, 96, 256), BF16),
            pltpu.VMEM((2, 2, 4, 8, 48, 384), BF16),
            pltpu.VMEM((BLK, D), F32),
            pltpu.VMEM((NB, BLK, D), BF16),
            pltpu.VMEM((NB, BLK, D), BF16),
            pltpu.VMEM((NB, BLK, 128), F32),
            pltpu.VMEM((NB, BLK, 128), F32),
            pltpu.VMEM((3 * BLK, 256), F32),
            pltpu.VMEM((ROWS + 32, 128), F32),
            pltpu.VMEM((12, ROWS, 128), F32),
            pltpu.VMEM((ROWS // 16, 16, D), BF16),
            pltpu.VMEM((2, 6, 1, 128), F32),
            pltpu.VMEM((16, 2, 6, 1, 128), F32),
            pltpu.VMEM((2, 6, 1, 128), F32),
            pltpu.VMEM((16, 2, 6, 1, 128), F32),
            pltpu.VMEM((2, 12, 1, 128), F32),
            dma, dma, dma, dma, dma((3,)), dma, dma, dma, dma, dma((3,)), dma((3,)), dma((3,)),
            dma((2,)), dma((2, 4)),
            dma, dma, dma, dma, dma, dma, dma, dma, dma, dma, dma, dma,
        ],
        compiler_params=pltpu.CompilerParams(
            collective_id=0, has_side_effects=True, vmem_limit_bytes=60 * 2**20
        ),
        cost_estimate=pl.CostEstimate(
            flops=20 * 10**9, bytes_accessed=10**7, transcendentals=4 * 10**6
        ),
    )(
        lengths.reshape(4), frames_in.reshape(CAP // 16, 16, D), norm_gain, norm_bias,
        w_in, w_out, taps, batch_gain, batch_bias,
        jnp.asarray(feature_order(), BF16), jnp.asarray(compaction(), BF16),
    )
    return out.reshape(1, CAP, D)


def solution(mesh):
    placed = (
        P("rep", "dp", None), P("rep", "dp", None), P(), P(), P(("dp", "rep"), None),
        P(), P(), P(), P(("dp", "rep"), None),
    )
    return jax.shard_map(
        on_device, mesh=mesh, in_specs=placed, out_specs=P("rep", "dp", None), check_vma=False
    )
```

```python
import functools

import jax
import jax.numpy as jnp
import numpy as np
from jax import lax
from jax.experimental import pallas as pl
from jax.experimental.pallas import tpu as pltpu
from jax.sharding import PartitionSpec as P

EPSILON = 1e-05
MESH = pl.DeviceIdType.MESH
F32 = jnp.float32
BF16 = jnp.bfloat16

NX, NY, NZ, NC = 4, 4, 8, 2
D = 1536
HALF = D // 2
CAP = 896
PAIR = 1024
GAP = 15
ROWS = 1152
BLK = 128
NB = ROWS // BLK
WIN = 192
TAPS = 31
N_IN = 6
TOTAL = 512 * 256


def feature_order():
    order = np.zeros((384, 384), np.float32)
    for z in range(8):
        for c in range(2):
            for y in range(4):
                for i in range(6):
                    order[z * 48 + c * 24 + y * 6 + i, y * 96 + z * 12 + c * 6 + i] = 1.0
    return order


def compaction():
    pick = np.zeros((96, 128), np.float32)
    for k in range(16):
        for i in range(6):
            pick[k * 6 + i, k * 8 + i] = 1.0
    return pick


def kernel(
    lengths_ref, x_ref, gain_1d, bias_1d, w_in_ref, w_out_ref, taps_ref, bgain_1d, bbias_1d,
    order_ref, pick_ref,
    out_ref,
    gain_ref, bias_ref, bgain_ref, bbias_ref, slab, slab_o, zin, both_o, zin_o, weights, wout, xs, normed_own, normed_mate, mask_own, mask_mate,
    proj, gated, conv, act, st_own, st_a, st_b0, st_b, stats,
    bo_send, bo_recv, z_send, zo_send, z_recv, zo_recv, r1_send, r2_send, r3_send, r1_recv, r2_recv, r3_recv,
    o_send, o_recv, n_send, n_recv, m_send, m_recv,
    c_send, c_recv, w_send, w_recv, sa_send, sa_recv, sb_send, sb_recv,
):
    dp = lax.axis_index("dp")
    y = lax.axis_index("rep")
    x = dp // 16
    z = lax.rem(dp // 2, 8)
    c = lax.rem(dp, 2)
    flips = [(1 - 2 * lax.rem(dp // 2**b, 2)) * 2**b for b in range(6)]
    y_flips = [(1 - 2 * lax.rem(y // 2**b, 2)) * 2**b for b in range(2)]

    def flip(start, deltas, k):
        for b, delta in enumerate(deltas):
            if k >> b & 1:
                start = start + delta
        return start

    mate = (flip(dp, flips, 1), y)
    z_peers = [(flip(dp, flips, k), y) for k in range(16)]
    xy_peers = [(flip(dp, flips, (k >> 2) << 4), flip(y, y_flips, k & 3)) for k in range(16)]
    zs_at = [lax.rem(z + k, 8) for k in range(8)]
    xs_at = [lax.rem(x + k, 4) for k in range(4)]
    ys_at = [lax.rem(y + k, 4) for k in range(4)]
    me_z = z * 2 + c
    me_xy = x * 4 + y

    barrier = pltpu.get_barrier_semaphore()
    for k in range(1, 16):
        pl.semaphore_signal(barrier, 1, device_id=z_peers[k], device_id_type=MESH)
        pl.semaphore_signal(barrier, 1, device_id=xy_peers[k], device_id_type=MESH)

    for vector, ref in (
        (gain_1d, gain_ref), (bias_1d, bias_ref), (bgain_1d, bgain_ref), (bbias_1d, bbias_ref)
    ):
        ref[...] = vector[...].reshape(1, D)

    slab[...] = jnp.zeros_like(slab)
    slab_o[...] = jnp.zeros_like(slab_o)
    for h in range(2):
        for j in range(N_IN):
            lo = h * HALF + j * 128
            slab[h, j // 2, j % 2, 0:6, 0:128] = w_in_ref[:, lo : lo + 128]
            slab[h, j // 2, j % 2, 0:6, 128:256] = w_in_ref[:, D + lo : D + lo + 128]
        for j in range(2):
            lo = h * HALF + j * 384
            slab_o[h, j, 0:6, :] = w_out_ref[:, lo : lo + 384]
    for p in range(3):
        zin[me_z, p] = slab[c, p]
    both_o[c] = slab_o[c]

    pl.semaphore_wait(barrier, 30)

    def send(src, dst, sent, landed, to):
        pltpu.make_async_remote_copy(
            src_ref=src, dst_ref=dst, send_sem=sent, recv_sem=landed,
            device_id=to, device_id_type=MESH,
        ).start()

    def wait_for(ref, sem):
        pltpu.make_async_copy(ref, ref, sem).wait()

    def s0(p):
        for k in range(1, 16):
            other = 1 - c if k % 2 else c
            part = pl.ds(p, 1 + p)
            send(slab.at[other, part], zin.at[me_z, part], z_send, z_recv.at[p], z_peers[k])

    def chunk(p, a):
        return weights.at[2 * p + a]

    def for_core(f):
        pl.when(c == 0)(lambda: f(0))
        pl.when(c == 1)(lambda: f(1))

    def s1(p):
        if p < 2:
            wait_for(zin.at[pl.ds(0, 15), pl.ds(0, 1 + p)], z_recv.at[p])
        for a in range(2):
            rows = zin[:, p, a].reshape(128, 256)
            chunk(p, a)[x, y] = jnp.dot(
                pick_ref[...], rows, preferred_element_type=F32
            ).astype(BF16)

        def go(v):
            for a in range(2):
                ref = chunk(p, a).at[x, y]
                for k in (1, 3, 2):
                    to = (dp + (xs_at[k] - x) * 16, y) if (v + a) % 2 == 0 else (dp, ys_at[k])
                    send(ref, ref, r1_send, r1_recv.at[p], to)

        for_core(go)

    def second(p, a, v, origin, part):
        if (v + a) % 2 == 0:
            return chunk(p, a).at[part, ys_at[origin]]
        return chunk(p, a).at[xs_at[origin], part]

    def second_to(a, v, k):
        return (dp, ys_at[k]) if (v + a) % 2 == 0 else (dp + (xs_at[k] - x) * 16, y)

    def s2(p):
        wait_for(chunk(p, 0).at[pl.ds(0, 2), pl.ds(0, 3)], r1_recv.at[p])

        def go(v):
            for a in range(2):
                ref = second(p, a, v, 0, pl.ds(0, 4))
                for k in (1, 3):
                    send(ref, ref, r2_send, r2_recv.at[p], second_to(a, v, k))

        for_core(go)

    def s3(p):
        wait_for(chunk(p, 0), r2_recv.at[p])

        def go(v):
            for a in range(2):
                for k, part in ((1, pl.ds(0, 2)), (3, pl.ds(2, 2))):
                    ref = second(p, a, v, 4 - k, part)
                    send(ref, ref, r3_send, r3_recv.at[p], second_to(a, v, k))

        for_core(go)

    def s4(p):
        wait_for(chunk(p, 0).at[pl.ds(0, 2)], r3_recv.at[p])

    def o0():
        wait_for(both_o.at[0], bo_recv)
        zin_o[x, :, y] = both_o[...]
        for k in range(1, 16):
            send(both_o, zin_o.at[x, :, y], zo_send, zo_recv, xy_peers[k])

    def bundle(a, k, part=pl.ds(0, 4)):
        return wout.at[c, a, part, zs_at[k]]

    def around(a, t, k, to, part=pl.ds(0, 4)):
        ref = bundle(a, k, part)
        send(ref, ref, o_send.at[0 if t < 3 else 1], o_recv.at[a, t], (dp + (zs_at[to] - z) * 2, y))

    def to_mate(a, k):
        send(bundle(a, k), bundle(a, k), w_send, w_recv, mate)

    def o1():
        wait_for(zin.at[pl.ds(0, 15)], zo_recv)
        for a in range(2):
            for g in range(2):
                rows = zin_o[2 * g : 2 * g + 2, :, :, a].reshape(128, 384)
                block = jnp.dot(pick_ref[...], rows, preferred_element_type=F32).astype(BF16)
                wout[c, a, 2 * g, z] = block[:48]
                wout[c, a, 2 * g + 1, z] = block[48:]
            around(a, 0, 0, 1)
            around(a, 0, 0, 7)
            to_mate(a, 0)

    def o2(t, a):
        wait_for(wout.at[0, a, :, pl.ds(0, 2)], o_recv.at[a, t - 1])
        if t < 3:
            around(a, t, 8 - t, 1)
            around(a, t, t, 7)
        else:
            around(a, t, 5, 1, pl.ds(0, 2))
            around(a, t, 3, 7, pl.ds(2, 2))
        to_mate(a, t)
        to_mate(a, 8 - t)

    def o3(a):
        wait_for(wout.at[0, a, :, 0], o_recv.at[a, 3])
        to_mate(a, 4)

    n_own = lengths_ref[0] + lengths_ref[1] + lengths_ref[2] + lengths_ref[3]
    b0 = lengths_ref[0]
    b1 = b0 + lengths_ref[1]
    b2 = b1 + lengths_ref[2]
    base = c * (PAIR - n_own + 4 * GAP)

    def place(i):
        u = (i >= b0).astype(jnp.int32) + (i >= b1).astype(jnp.int32) + (i >= b2).astype(jnp.int32)
        return i + base + GAP * u

    def window(ref, w):
        return jnp.concatenate([ref[w + k] for k in range(WIN // 16)], axis=0)

    def layer_norm_block(qi):
        q = qi + c
        low = jnp.maximum(q * BLK - base - 3 * GAP, 0)
        w = jnp.minimum(lax.div(low, 16), (CAP - WIN) // 16)
        i = w * 16 + lax.broadcasted_iota(jnp.int32, (BLK, WIN), 1)
        r = q * BLK + lax.broadcasted_iota(jnp.int32, (BLK, WIN), 0)
        chosen = jnp.logical_and(place(i) == r, i < n_own).astype(F32)
        xs[...] = jnp.dot(chosen.astype(BF16), window(x_ref, w), preferred_element_type=F32)
        live = jnp.broadcast_to(jnp.sum(chosen, axis=1, keepdims=True), (BLK, 128))
        mask_own[q] = live

        def rows(g, carry):
            at = pl.ds(pl.multiple_of(g * 16, 16), 16)
            v = xs[at, :]
            average = jnp.sum(v, axis=1, keepdims=True) * (1.0 / D)
            centred = v - average
            spread = jnp.sum(centred * centred, axis=1, keepdims=True) * (1.0 / D)
            res = centred * lax.rsqrt(spread + EPSILON) * gain_ref[...] + bias_ref[...]
            m = mask_own[q, at, 0:1]
            normed_own[q, at, :] = jnp.where(m > 0.0, res, 0.0).astype(BF16)
            return carry

        lax.fori_loop(0, BLK // 16, rows, 0, unroll=4)
        pltpu.make_async_remote_copy(
            src_ref=normed_own.at[q], dst_ref=normed_mate.at[q], send_sem=n_send, recv_sem=n_recv,
            device_id=mate, device_id_type=MESH,
        ).start()

    def project(j):
        w = weights[j].reshape(D, 256)

        def rows(b, carry):
            at = pl.ds(0, 9)
            proj[...] = jnp.dot(
                normed_own[at].reshape(9 * BLK, D), w, preferred_element_type=F32
            )
            v = proj[:, 0:128]
            g = proj[:, 128:256]
            res = v * jax.nn.sigmoid(g)
            gated[pl.ds(16, 9 * BLK), :] = res.astype(BF16).astype(F32)
            return carry

        rows(0, 0)

    def convolve(j):
        cc = c * N_IN + j
        lanes = pl.ds(pl.multiple_of(cc * 128, 128), 128)
        taps = taps_ref[:, lanes]

        def rows(b, total):
            r0 = pl.multiple_of(b * BLK, BLK)
            v = gated[pl.ds(r0, BLK + 32), :]
            acc = jnp.zeros((BLK, 128), F32)
            for r in range(8):
                turned = v if r == 0 else pltpu.roll(v, BLK + 32 - r, axis=0)
                for m in range(4):
                    o = 8 * m + r - 1
                    if 0 <= o < TAPS:
                        acc = acc + turned[8 * m : 8 * m + BLK] * taps[o : o + 1]
            acc = acc * mask_own[b]
            conv[cc, pl.ds(r0, BLK), :] = acc
            return total + jnp.sum(acc.reshape(BLK // 8, 8, 128), axis=0)

        total = lax.fori_loop(0, NB, rows, jnp.zeros((8, 128), F32))
        average = jnp.sum(total, axis=0, keepdims=True) * (1.0 / PAIR)

        def deviations(b, total):
            r0 = pl.multiple_of(b * BLK, BLK)
            diff = (conv[cc, pl.ds(r0, BLK), :] - average) * mask_own[b]
            return total + jnp.sum((diff * diff).reshape(BLK // 8, 8, 128), axis=0)

        square = lax.fori_loop(0, NB, deviations, jnp.zeros((8, 128), F32))
        st_own[0, j] = average
        st_own[1, j] = jnp.sum(square, axis=0, keepdims=True)
        at = pl.ds(pl.multiple_of((1 - c) * BLK, BLK), PAIR)
        pltpu.make_async_remote_copy(
            src_ref=conv.at[cc, at], dst_ref=conv.at[cc, at], send_sem=c_send, recv_sem=c_recv,
            device_id=mate, device_id_type=MESH,
        ).start()

    def loop(lo, hi, f):
        lax.fori_loop(lo, hi, lambda k, carry: (f(k), carry)[1], 0)

    gated[0:16, :] = jnp.zeros((16, 128), F32)
    gated[ROWS + 16 : ROWS + 32, :] = jnp.zeros((16, 128), F32)

    send(slab_o.at[1 - c], both_o.at[c], bo_send, bo_recv, mate)
    s0(0)
    s0(1)
    normed_own[8 * (1 - c)] = jnp.zeros((BLK, D), BF16)
    mask_own[8 * (1 - c)] = jnp.zeros((BLK, 128), F32)
    normed_mate[8 * c] = jnp.zeros((BLK, D), BF16)
    mask_mate[8 * c] = jnp.zeros((BLK, 128), F32)

    def norm_step(i):
        layer_norm_block(i)

        for at, steps in (
            (0, (o0,)),
            (2, (lambda: s1(0),)),
            (6, (lambda: s2(0), lambda: s1(1))),
        ):
            @pl.when(i == at)
            def _(steps=steps):
                for step in steps:
                    step()

    loop(0, 8, norm_step)
    masks = pl.ds(c, 8)
    send(mask_own.at[masks], mask_mate.at[masks], m_send, m_recv, mate)
    wait_for(normed_mate.at[pl.ds(0, 8)], n_send)
    wait_for(mask_mate.at[pl.ds(0, 8)], m_send)
    wait_for(normed_mate.at[pl.ds(0, 8)], n_recv)
    wait_for(mask_mate.at[pl.ds(0, 8)], m_recv)

    def join(b):
        at = pl.ds(b * 3, 3)
        both = (normed_own[at] + normed_mate[at]).reshape(3 * BLK, D)
        for g in range(4):
            cols = slice(g * 384, (g + 1) * 384)
            normed_own[at, :, cols] = jnp.dot(
                both[:, cols], order_ref[...], preferred_element_type=F32
            ).astype(BF16).reshape(3, BLK, 384)
        mask_own[at] = mask_own[at] + mask_mate[at]

    def join_step(b):
        join(b)

        @pl.when(b == 0)
        def _():
            o1()

    loop(0, NB // 3, join_step)
    s3(0)
    s2(1)
    s1(2)
    o2(1, 0)
    s4(0)

    def compute(j):
        project(j)
        for at, steps in (
            (0, (lambda: o2(1, 1),)), (1, (lambda: o2(2, 1),)),
            (2, (lambda: s3(2),)), (3, (lambda: o2(3, 1),)), (5, (lambda: o3(1),)),
        ):
            @pl.when(j == at)
            def _(steps=steps):
                for step in steps:
                    step()
        convolve(j)
        for at, steps in (
            (0, (lambda: s3(1), lambda: s2(2), lambda: o2(2, 0))), (1, (lambda: s4(1),)),
            (2, (lambda: o2(3, 0),)), (3, (lambda: s4(2),)), (4, (lambda: o3(0),)),
        ):
            @pl.when(j == at)
            def _(steps=steps):
                for step in steps:
                    step()

    loop(0, N_IN, compute)

    st_a[me_xy] = st_own[...]
    for k in range(1, 16):
        send(st_own, st_a.at[me_xy], sa_send, sa_recv, xy_peers[k])
    wait_for(st_a.at[pl.ds(0, 15)], sa_recv)
    all_a = st_a[...]
    mean_a = jnp.sum(all_a[:, 0], axis=0) * (1.0 / 16)
    off_a = all_a[:, 0] - mean_a[None]
    st_b0[0] = mean_a
    st_b0[1] = jnp.sum(all_a[:, 1], axis=0) + PAIR * jnp.sum(off_a * off_a, axis=0)
    me_b = c * 8 + z
    st_b[me_b] = st_b0[...]
    for k in range(1, 16):
        send(st_b0, st_b.at[me_b], sb_send, sb_recv, z_peers[k])
    wait_for(st_b.at[pl.ds(0, 15)], sb_recv)
    for h in range(2):
        part = st_b[h * 8 : h * 8 + 8]
        mean_b = jnp.sum(part[:, 0], axis=0) * (1.0 / 8)
        off_b = part[:, 0] - mean_b[None]
        spread = (
            jnp.sum(part[:, 1], axis=0) + (16 * PAIR) * jnp.sum(off_b * off_b, axis=0)
        ) * (1.0 / TOTAL)
        stats[0, h * 6 : h * 6 + 6] = mean_b
        stats[1, h * 6 : h * 6 + 6] = lax.rsqrt(spread + EPSILON)

    at_mine = pl.ds(pl.multiple_of(c * BLK, BLK), PAIR)
    wait_for(conv.at[pl.ds(0, 6), pl.ds(0, PAIR)], c_recv)
    wait_for(wout.at[0], w_recv)

    def activate(qi):
        q = qi + c
        at = pl.ds(pl.multiple_of(q * BLK, BLK), BLK)
        for cc in range(12):
            lanes = slice(cc * 128, cc * 128 + 128)
            v = conv[cc, at, :] - stats[0, cc]
            v = v * (stats[1, cc] * bgain_ref[:, lanes]) + bbias_ref[:, lanes]
            act[pl.ds(q * 8, 8), :, lanes] = jax.nn.silu(v).astype(BF16).reshape(8, 16, 128)

    loop(0, 8, activate)

    def finish(t):
        i0 = t * BLK
        low = base + i0
        w = jnp.minimum(lax.div(low, 16), (ROWS - WIN) // 16)
        i = i0 + lax.broadcasted_iota(jnp.int32, (BLK, WIN), 0)
        r = w * 16 + lax.broadcasted_iota(jnp.int32, (BLK, WIN), 1)
        chosen = jnp.logical_and(place(i) == r, i < n_own).astype(F32).astype(BF16)
        mine = jnp.dot(chosen, window(act, w), preferred_element_type=F32).astype(BF16)
        rows = pl.ds(t * 8, 8)
        live = i0 + lax.broadcasted_iota(jnp.int32, (BLK, 384), 0) < n_own
        for h in range(2):
            for k in range(2):
                lo = h * HALF + k * 384
                branch = jnp.dot(
                    mine, wout[h, k].reshape(D, 384), preferred_element_type=F32
                )
                res = x_ref[rows, :, lo : lo + 384].reshape(BLK, 384).astype(F32) + branch
                out_ref[rows, :, lo : lo + 384] = jnp.where(live, res, 0.0).astype(BF16).reshape(8, 16, 384)

    loop(0, CAP // BLK, finish)

    wait_for(zin.at[pl.ds(0, 15)], z_send)
    wait_for(both_o.at[0], bo_send)
    wait_for(zin.at[pl.ds(0, 15)], zo_send)
    wait_for(weights.at[:, pl.ds(0, 3), 0], r1_send)
    wait_for(weights.at[pl.ds(0, 3)], r2_send)
    wait_for(weights.at[:, 0], r3_send)
    wait_for(wout.at[0, :, :, pl.ds(0, 6)], o_send.at[0])
    wait_for(wout.at[0, :, :, 0], o_send.at[1])
    wait_for(conv.at[pl.ds(0, 6), pl.ds(0, PAIR)], c_send)
    wait_for(wout.at[0], w_send)
    wait_for(st_a.at[pl.ds(0, 15)], sa_send)
    wait_for(st_b.at[pl.ds(0, 15)], sb_send)


def on_device(
    frames_in, lengths, norm_gain, norm_bias, w_in, taps, batch_gain, batch_bias, w_out
):
    vmem = pl.BlockSpec(memory_space=pltpu.VMEM)
    dma = pltpu.SemaphoreType.DMA
    out = pl.pallas_call(
        kernel,
        out_shape=jax.ShapeDtypeStruct((CAP // 16, 16, D), BF16),
        in_specs=[pl.BlockSpec(memory_space=pltpu.SMEM)] + [vmem] * 10,
        out_specs=vmem,
        scratch_shapes=[
            pltpu.VMEM((1, D), F32), pltpu.VMEM((1, D), F32),
            pltpu.VMEM((1, D), F32), pltpu.VMEM((1, D), F32),
            pltpu.VMEM((2, 3, 2, 8, 256), BF16),
            pltpu.VMEM((2, 2, 8, 384), BF16),
            pltpu.VMEM((16, 3, 2, 8, 256), BF16),
            pltpu.VMEM((2, 2, 8, 384), BF16),
            pltpu.VMEM((4, 2, 4, 2, 8, 384), BF16),
            pltpu.VMEM((N_IN, 4, 4, 96, 256), BF16),
            pltpu.VMEM((2, 2, 4, 8, 48, 384), BF16),
            pltpu.VMEM((BLK, D), F32),
            pltpu.VMEM((NB, BLK, D), BF16),
            pltpu.VMEM((NB, BLK, D), BF16),
            pltpu.VMEM((NB, BLK, 128), F32),
            pltpu.VMEM((NB, BLK, 128), F32),
            pltpu.VMEM((9 * BLK, 256), F32),
            pltpu.VMEM((ROWS + 32, 128), F32),
            pltpu.VMEM((12, ROWS, 128), F32),
            pltpu.VMEM((ROWS // 16, 16, D), BF16),
            pltpu.VMEM((2, 6, 1, 128), F32),
            pltpu.VMEM((16, 2, 6, 1, 128), F32),
            pltpu.VMEM((2, 6, 1, 128), F32),
            pltpu.VMEM((16, 2, 6, 1, 128), F32),
            pltpu.VMEM((2, 12, 1, 128), F32),
            dma, dma, dma, dma, dma((3,)), dma, dma, dma, dma, dma((3,)), dma((3,)), dma((3,)),
            dma((2,)), dma((2, 4)),
            dma, dma, dma, dma, dma, dma, dma, dma, dma, dma, dma, dma,
        ],
        compiler_params=pltpu.CompilerParams(
            collective_id=0, has_side_effects=True, vmem_limit_bytes=60 * 2**20
        ),
        cost_estimate=pl.CostEstimate(
            flops=20 * 10**9, bytes_accessed=10**7, transcendentals=4 * 10**6
        ),
    )(
        lengths.reshape(4), frames_in.reshape(CAP // 16, 16, D), norm_gain, norm_bias,
        w_in, w_out, taps, batch_gain, batch_bias,
        jnp.asarray(feature_order(), BF16), jnp.asarray(compaction(), BF16),
    )
    return out.reshape(1, CAP, D)


def solution(mesh):
    placed = (
        P("rep", "dp", None), P("rep", "dp", None), P(), P(), P(("dp", "rep"), None),
        P(), P(), P(), P(("dp", "rep"), None),
    )
    return jax.shard_map(
        on_device, mesh=mesh, in_specs=placed, out_specs=P("rep", "dp", None), check_vma=False
    )
```
